512 devices in a mesh: edp: 16 (over z, core), ep: 32 (over y, x).
Axes of the slice: x: 4, y: 8, z: 8, core: 2. Of those that a mesh axis runs over, the one named last changes fastest.
Arguments:
- token_acts: bfloat16 [16, 32, 2, 64, 1024], P('edp', 'ep'), may hold values from -6 to 6
- out_grad: bfloat16 [16, 32, 3584, 128], P('edp', 'ep'), may hold values from -0.59765625 to 0.59765625
- counts: int32 [16, 32, 2], P('edp', 'ep'), may hold values from 1 to 64, as said below
- params: float32 [32, 3584, 1024], P('ep', 'edp'), may hold values from -3 to 3
- first_moment: bfloat16 [32, 3584, 1024], P('ep', 'edp'), may hold values from -3 to 3
- second_moment: bfloat16 [32, 3584, 1024], P('ep', 'edp'), may hold values from 0.049804688 to 2
- old_expert: int32 [32], replicated, may hold values from 0 to 31, each once
- replica_of: int32 [32], replicated, may hold values from 0 to 31
- new_expert: int32 [32], replicated, may hold values from 0 to 31, each once
Outputs:
- update_step: float32 [32, 3584, 1024], P('ep', 'edp')
- new_first: bfloat16 [32, 3584, 1024], P('ep', 'edp')
- new_second: bfloat16 [32, 3584, 1024], P('ep', 'edp')
The draws below stay inside these ranges and needn't reach their ends.
Inputs may be any that keep to these rules, and one draw needn't show every extreme that they name: `counts`: every slot has at least one live token; some slot is full and some slot has exactly one live token in every draw. `old_expert`: each expert appears exactly once. `new_expert`: each expert appears exactly once. `replica_of`: any expert may be served by any number of replica slots, its owner's included.
All inputs are finite; a program needn't handle non-finite values.
Results may differ from the reference program's by a relative error of at most 0.015.
Values may be sent and summed in bfloat16 or wider, within the bound.
A program may use at most 64 MiB of HBM per device.

```python
import math
import jax
import jax.numpy as jnp
import numpy as np
from jax import lax

D = 3584
FF = 1024
TOK = 64
SLOTS = 2
GROUPS = 16
EXPERTS = 32


def draw_counts(key, part):
    total = GROUPS * EXPERTS * SLOTS
    key_base = jax.random.fold_in(key, 11)
    key_full = jax.random.fold_in(key, 12)
    key_single = jax.random.fold_in(key, 13)
    base = jax.random.randint(key_base, (total,), 1, TOK + 1, dtype=jnp.int32)
    full_at = jax.random.randint(key_full, (), 0, total, dtype=jnp.int32)
    offset = jax.random.randint(key_single, (), 1, total, dtype=jnp.int32)
    single_at = (full_at + offset) % total
    index = jnp.arange(total, dtype=jnp.int32)
    filled = jnp.where(index == full_at, TOK, base)
    filled = jnp.where(index == single_at, 1, filled)
    return filled.reshape(GROUPS, EXPERTS, SLOTS).astype(jnp.int32)


def plant(entries, own_key, low, top_value):
    extent = entries.shape
    index_at = [jax.random.randint(jax.random.fold_in(own_key, axis), (), 0, extent[axis]) for axis in range(len(extent))]
    entries = entries.at[tuple(index_at)].set(low)
    longest = extent.index(max(extent))
    index_at[longest] = (index_at[longest] + 1) % extent[longest]
    return entries.at[tuple(index_at)].set(top_value)


def levels(rng, dims, cuts, least, top_value):
    factor_of = 1.0
    for axis_at, blocks in cuts:
        draws = jax.random.uniform(jax.random.fold_in(jax.random.fold_in(rng, 6), axis_at), (blocks,), jnp.float32, least / len(cuts), top_value / len(cuts))
        factor_of = factor_of * jnp.repeat(jnp.exp(draws), dims[axis_at] // blocks).reshape((-1,) + (1,) * (len(dims) - 1 - axis_at))
    return factor_of


def rank_bounds(amount, skew):
    portions = [(1 << 20) // math.isqrt(rank ** skew) + 1 for rank in range(1, amount + 1)]
    spread = 1 + sum(portions) // (1 << 30)
    return np.cumsum(np.array([max(1, weight // spread) for weight in portions]))


def ranked_ids(own_key, extent, count, skew):
    grid = rank_bounds(count, skew)
    pick = jax.random.randint(jax.random.fold_in(own_key, 1), extent, 0, int(grid[count - 1]))
    rank = jnp.searchsorted(jnp.asarray(grid, jnp.int32), pick, side="right")
    return jax.random.permutation(jax.random.fold_in(own_key, 2), count)[rank].astype(jnp.int32)


def noise(rng, shape, spread, bound, shards=(), kind=jnp.bfloat16):
    array = spread * jax.random.normal(rng, shape, jnp.float32)
    if shards:
        array = array * levels(rng, shape, shards, -0.22, 0.18)
    return jnp.clip(array, -bound, bound).astype(kind)


def setup_inputs(seed: int = 0) -> dict:
    key_of = jax.random.split(jax.random.key(seed), 10)
    return {
        "token_acts": noise(key_of[0], (GROUPS, EXPERTS, SLOTS, TOK, FF), 1.0, 6.0, ((0, 16), (1, 32))),
        "out_grad": noise(key_of[1], (GROUPS, EXPERTS, D, SLOTS * TOK), 0.1, 0.59765625, ((0, 16), (1, 32))),
        "counts": draw_counts(jax.random.fold_in(key_of[9], 71), 0),
        "params": noise(key_of[3], (EXPERTS, D, FF), 0.5, 3.0, ((0, 32), (1, 16)), jnp.float32),
        "first_moment": noise(key_of[4], (EXPERTS, D, FF), 0.5, 3.0, ((0, 32), (1, 16))),
        "second_moment": jnp.clip(jnp.exp(math.log(2.0) - 3.6927934 * jax.random.uniform(key_of[5], (EXPERTS, D, FF), jnp.float32) ** levels(key_of[5], (EXPERTS, D, FF), ((0, 32), (1, 16)), -0.2, 0.2)), 0.049804688, 2.0).astype(jnp.bfloat16),
        "old_expert": jax.random.permutation(key_of[6], EXPERTS).astype(jnp.int32),
        "replica_of": plant(ranked_ids(key_of[7], (EXPERTS,), EXPERTS, 2), jax.random.fold_in(key_of[7], 3), 0, EXPERTS - 1).astype(jnp.int32),
        "new_expert": jax.random.permutation(key_of[8], EXPERTS).astype(jnp.int32),
    }


beta_one = 0.9
beta_two = 0.95
bias_one = 0.9999734386011124
bias_two = 0.994079470779666
decay_rate = 0.1
adam_eps = 1e-08

def adam_update(weights, first_old, second_old, gradient):
    first_new = beta_one * first_old.astype(jnp.float32) + (1.0 - beta_one) * gradient
    second_new = beta_two * second_old.astype(jnp.float32) + (1.0 - beta_two) * gradient * gradient
    scaled = first_new / bias_one / (jnp.sqrt(second_new / bias_two) + adam_eps)
    step_new = -(scaled + decay_rate * weights)
    return (step_new, first_new.astype(jnp.bfloat16), second_new.astype(jnp.bfloat16))

def reference(token_acts, out_grad, counts, params, first_moment, second_moment, old_expert, replica_of, new_expert):
    column = jnp.arange(SLOTS * TOK, dtype=jnp.int32)
    position = column % TOK
    slot_index = column // TOK
    live_limit = counts[:, :, slot_index]
    live_mask = position[None, None, :] < live_limit
    live_grad = jnp.where(live_mask[:, :, None, :], out_grad, jnp.zeros_like(out_grad))

    def slot_grads(expert_index):
        grad_block = live_grad[:, expert_index].astype(jnp.float32).reshape(GROUPS, D, SLOTS, TOK)
        acts_block = token_acts[:, expert_index].astype(jnp.float32)
        return jnp.einsum('gdst,gstf->sdf', grad_block, acts_block, precision=lax.Precision.HIGHEST)
    all_grads = lax.map(slot_grads, jnp.arange(EXPERTS, dtype=jnp.int32))
    own_grad = all_grads[:, 0]
    replica_grad = all_grads[:, 1]
    sum_matrix = (replica_of[None, :] == old_expert[:, None]).astype(jnp.float32)
    summed_grad = own_grad + jnp.einsum('st,tdf->sdf', sum_matrix, replica_grad, precision=lax.Precision.HIGHEST)
    step_new, first_new, second_new = adam_update(params, first_moment, second_moment, summed_grad)
    inverse = jnp.zeros((EXPERTS,), jnp.int32).at[old_expert].set(jnp.arange(EXPERTS, dtype=jnp.int32))
    source = inverse[new_expert]
    return (jnp.take(step_new, source, axis=0), jnp.take(first_new, source, axis=0), jnp.take(second_new, source, axis=0))
```

```python
import functools

import jax
import jax.numpy as jnp
from jax import lax
from jax.experimental import pallas as pl
from jax.experimental.pallas import tpu as pltpu
from jax.sharding import PartitionSpec as P

beta_one = 0.9
beta_two = 0.95
bias_one = 0.9999734386011124
bias_two = 0.994079470779666
decay_rate = 0.1
adam_eps = 1e-08

LANES = 128
SUB = 8
MESH = pl.DeviceIdType.MESH
BF = jnp.bfloat16
F32 = jnp.float32


def splits(rows):
    first = 32 if rows > 32 else rows
    return [(0, first)] + ([(first, rows - first)] if rows > first else [])


def kernel(groups, owners, *refs):
    (acts_ref, grad_ref, counts_ref, p_ref, f_ref, s_ref, old_ref, rep_ref, new_ref) = refs[:9]
    step_ref, first_ref, second_ref = refs[9:12]
    rest = list(refs[12:])
    acts_all, p_v, f_v, s_v, st, st_in, pick, placed, step_v, first_v, second_v = rest[:11]
    rest = rest[11:]
    parts, rows, hidden = p_ref.shape
    cols = hidden // LANES
    tokens = acts_ref.shape[0]
    half = tokens // 2
    chunks = splits(rows)
    n_chunks = len(chunks)
    g_buf, gs, gi, os_, oi = (rest[i * n_chunks : (i + 1) * n_chunks] for i in range(5))
    rest = rest[5 * n_chunks :]
    (load_sem, g_sem, ring_send, ring_recv, pair_send, pair_recv, a_send, st_sem, gr_sem, out_sem) = rest

    r = lax.axis_index("edp")
    e = lax.axis_index("ep")
    chips = groups // 2
    core = lax.rem(r, 2)
    z = r // 2

    barrier = pltpu.get_barrier_semaphore()

    def greet_group(k, _):
        pl.semaphore_signal(
            barrier, inc=1, device_id=(lax.rem(r + k, groups), e), device_id_type=MESH
        )
        return 0

    def greet_owner(k, _):
        pl.semaphore_signal(
            barrier, inc=1, device_id=(r, lax.rem(e + k, owners)), device_id_type=MESH
        )
        return 0

    lax.fori_loop(1, groups, greet_group, 0)
    lax.fori_loop(1, owners, greet_owner, 0)

    own_acts = acts_all.at[r]
    load_acts = pltpu.make_async_copy(acts_ref, own_acts, load_sem.at[0])
    load_p = pltpu.make_async_copy(p_ref, p_v, load_sem.at[1])
    load_f = pltpu.make_async_copy(f_ref, f_v, load_sem.at[2])
    load_s = pltpu.make_async_copy(s_ref, s_v, load_sem.at[3])
    load_acts.start()
    load_p.start()
    load_f.start()
    load_s.start()

    load_acts.wait()
    token = lax.broadcasted_iota(jnp.int32, (half, hidden), 0)
    for slot in range(2):
        block = acts_all[r, slot * half : (slot + 1) * half, :].astype(F32)
        live = jnp.where(token < counts_ref[slot], block, 0.0)
        acts_all[r, slot * half : (slot + 1) * half, :] = live.astype(BF)

    pl.semaphore_wait(barrier, groups - 1 + owners - 1)

    def send_rows(i):
        first, size = chunks[i]
        lanes = pl.ds(pl.multiple_of(r * LANES, LANES), LANES)

        def body(k, _):
            to = lax.rem(r + k, groups)
            pltpu.make_async_remote_copy(
                src_ref=grad_ref.at[to, :, first : first + size, :],
                dst_ref=g_buf[i].at[:, :, lanes],
                send_sem=a_send.at[i],
                recv_sem=g_sem.at[i],
                device_id=(to, e),
                device_id_type=MESH,
            ).start()
            return 0

        lax.fori_loop(1, groups, body, 0)
        pltpu.make_async_copy(
            grad_ref.at[r, :, first : first + size, :], g_buf[i].at[:, :, lanes], g_sem.at[i]
        ).start()

    def ring(direction, hop, h):
        away = hop if direction == 0 else chips - hop
        block = lax.rem(z + chips - away, chips) * 2 + core
        to = lax.rem(z + (1 if direction == 0 else chips - 1), chips) * 2 + core
        ref = acts_all.at[block, pl.ds(h * half, half), :]
        return pltpu.make_async_remote_copy(
            src_ref=ref,
            dst_ref=ref,
            send_sem=ring_send.at[direction, hop, h],
            recv_sem=ring_recv.at[direction, hop, h],
            device_id=(to, e),
            device_id_type=MESH,
        )

    def arrived(direction, hop, h):
        away = hop + 1 if direction == 0 else chips - hop - 1
        block = lax.rem(z + chips - away, chips) * 2 + core
        ref = acts_all.at[block, pl.ds(h * half, half), :]
        return ref, pltpu.make_async_copy(ref, ref, ring_recv.at[direction, hop, h])

    def to_pair(ref):
        pltpu.make_async_remote_copy(
            src_ref=ref,
            dst_ref=ref,
            send_sem=pair_send,
            recv_sem=pair_recv,
            device_id=(r + 1 - 2 * core, e),
            device_id_type=MESH,
        ).start()

    far = chips // 2

    def goes(direction, hop, h):
        return hop < far - 1 or (hop == far - 1 and h == direction)

    ring_ops = [
        (direction, hop, h)
        for hop in range(far)
        for h in (0, 1)
        for direction in (0, 1)
        if goes(direction, hop, h)
    ]

    def spread(buf, landing, send_sem, recv_sem):
        def body(k, _):
            to = lax.rem(e + k, owners)
            pltpu.make_async_remote_copy(
                src_ref=buf.at[to],
                dst_ref=landing.at[e],
                send_sem=send_sem,
                recv_sem=recv_sem,
                device_id=(r, to),
                device_id_type=MESH,
            ).start()
            return 0

        lax.fori_loop(1, owners, body, 0)
        pltpu.make_async_copy(buf.at[e], landing.at[e], recv_sem).start()

    def wait_all(ref, sem):
        pltpu.make_async_copy(ref, ref, sem).wait()

    send_rows(0)
    for op in ring_ops:
        if op[1] == 0:
            ring(*op).start()
    to_pair(own_acts)

    load_p.wait()
    load_f.wait()
    load_s.wait()
    for q in range(parts):
        for c in range(cols):
            lanes = slice(c * LANES, (c + 1) * LANES)
            st[q * cols + c, 0] = p_v[q, :, lanes].astype(BF)
            st[q * cols + c, 1] = f_v[q, :, lanes]
            st[q * cols + c, 2] = s_v[q, :, lanes]
    spread(st, st_in, st_sem.at[0], st_sem.at[1])

    wide = SUB * owners
    lane = lax.broadcasted_iota(jnp.int32, (SUB, wide), 1)
    sub = lax.broadcasted_iota(jnp.int32, (SUB, wide), 0)
    same_row = lax.rem(lane, SUB) == sub
    lane_expert = lane // SUB
    old_wide = jnp.zeros((SUB, wide), jnp.int32)
    rep_wide = jnp.zeros((SUB, wide), jnp.int32)
    for i in range(owners):
        old_wide = jnp.where(lane_expert == i, old_ref[i], old_wide)
        rep_wide = jnp.where(lane_expert == i, rep_ref[i], rep_wide)
    for d in range(owners):
        at = slice(d * SUB, (d + 1) * SUB)
        pick[at, :wide] = jnp.where(same_row & (old_wide == new_ref[d]), 1.0, 0.0)
        pick[at, wide:] = jnp.where(same_row & (rep_wide == new_ref[d]), 1.0, 0.0)

    for direction, hop, h in ring_ops:
        ref, copy = arrived(direction, hop, h)
        copy.wait()
        if hop + 1 < far and goes(direction, hop + 1, h):
            ring(direction, hop + 1, h).start()
        to_pair(ref)
    for i in range(1, n_chunks):
        send_rows(i)
    for direction, hop, h in ring_ops:
        ring(direction, hop, h).wait_send()
    mine = acts_all.at[pl.ds(0, chips)]
    wait_all(mine, pair_recv)

    def gradients(i):
        first, size = chunks[i]
        wait_all(g_buf[i], g_sem.at[i])
        width = groups * LANES
        block = g_buf[i][...].astype(F32).reshape(parts * size, width)
        in_own = lax.rem(lax.broadcasted_iota(jnp.int32, block.shape, 1), LANES) < LANES // 2
        left = jnp.concatenate(
            [jnp.where(in_own, block, 0.0).astype(BF), jnp.where(in_own, 0.0, block).astype(BF)], 0
        )
        for c0 in range(0, hidden, 256):
            n = min(256, hidden - c0)
            right = acts_all[:, :, c0 : c0 + n].reshape(groups * tokens, n)
            out = jnp.dot(left, right, preferred_element_type=F32)
            for slot in range(2):
                for q in range(parts):
                    at = (slot * parts + q) * size
                    for c in range(n // LANES):
                        piece = out[at : at + size, c * LANES : (c + 1) * LANES]
                        gs[i][q * cols + c0 // LANES + c, slot] = piece.astype(BF)
        spread(gs[i], gi[i], gr_sem.at[0, i], gr_sem.at[1, i])

    for i in range(n_chunks):
        gradients(i)

    def stack(ref, item, at):
        return ref[:, item, at : at + SUB, :].astype(F32).reshape(wide, LANES).astype(BF)

    wait_all(st_in, st_sem.at[1])
    move = pick[:, :wide].astype(BF)
    for t in range(rows // SUB):
        state = jnp.concatenate([stack(st_in, item, t * SUB) for item in range(3)], 1)
        placed[t] = jnp.dot(move, state, preferred_element_type=F32)

    def update(i):
        first, size = chunks[i]
        wait_all(gi[i], gr_sem.at[1, i])
        both = pick[...].astype(BF)
        for t in range(size // SUB):
            at = t * SUB
            terms = jnp.concatenate([stack(gi[i], 0, at), stack(gi[i], 1, at)], 0)
            gradient = jnp.dot(both, terms, preferred_element_type=F32)
            old = placed[first // SUB + t]
            weights, first_old, second_old = (old[:, k * LANES : (k + 1) * LANES] for k in range(3))
            first_new = beta_one * first_old + (1.0 - beta_one) * gradient
            second_new = beta_two * second_old + (1.0 - beta_two) * gradient * gradient
            scaled = first_new / bias_one / (jnp.sqrt(second_new / bias_two) + adam_eps)
            step = -(scaled + decay_rate * weights)
            for item, value in enumerate((step, first_new, second_new)):
                os_[i][:, item, at : at + SUB, :] = value.reshape(owners, SUB, LANES).astype(BF)
        spread(os_[i], oi[i], out_sem.at[0, i], out_sem.at[1, i])

    for i in range(n_chunks):
        update(i)

    for i in range(n_chunks):
        first, size = chunks[i]
        wait_all(oi[i], out_sem.at[1, i])
        at = slice(first, first + size)
        for q in range(parts):
            for c in range(cols):
                lanes = slice(c * LANES, (c + 1) * LANES)
                step_v[q, at, lanes] = oi[i][q * cols + c, 0].astype(F32)
                first_v[q, at, lanes] = oi[i][q * cols + c, 1]
                second_v[q, at, lanes] = oi[i][q * cols + c, 2]
    stores = [
        pltpu.make_async_copy(a, b, load_sem.at[k])
        for k, (a, b) in enumerate(
            ((step_v, step_ref), (first_v, first_ref), (second_v, second_ref))
        )
    ]
    for s in stores:
        s.start()

    wait_all(mine, pair_send)
    others = pl.ds(0, owners - 1)
    wait_all(st.at[others], st_sem.at[0])
    for i in range(n_chunks):
        wait_all(g_buf[i].at[:, :, pl.ds(0, (groups - 1) * LANES)], a_send.at[i])
        wait_all(gs[i].at[others], gr_sem.at[0, i])
        wait_all(os_[i].at[others], out_sem.at[0, i])
    for s in stores:
        s.wait()


def local(groups, owners, token_acts, out_grad, counts, params, first, second, old, rep, new):
    model_width, width = out_grad.shape[2:]
    slot_count, tok, hidden = token_acts.shape[2:]
    row_count = model_width // groups
    cols = hidden // LANES
    parts = owners // cols
    rows = row_count // parts
    chunks = splits(rows)
    block = (parts, rows, hidden)
    any_spec = pl.BlockSpec(memory_space=pl.ANY)
    smem = pl.BlockSpec(memory_space=pltpu.SMEM)
    n = len(chunks)
    wide = SUB * owners
    dma = pltpu.SemaphoreType.DMA
    out = pl.pallas_call(
        functools.partial(kernel, groups, owners),
        out_shape=[
            jax.ShapeDtypeStruct(block, F32),
            jax.ShapeDtypeStruct(block, BF),
            jax.ShapeDtypeStruct(block, BF),
        ],
        in_specs=[any_spec, any_spec, smem, any_spec, any_spec, any_spec, smem, smem, smem],
        out_specs=[any_spec] * 3,
        scratch_shapes=[
            pltpu.VMEM((groups, slot_count * tok, hidden), BF),
            pltpu.VMEM(block, F32),
            pltpu.VMEM(block, BF),
            pltpu.VMEM(block, BF),
            pltpu.VMEM((owners, 3, rows, LANES), BF),
            pltpu.VMEM((owners, 3, rows, LANES), BF),
            pltpu.VMEM((wide, 2 * wide), F32),
            pltpu.VMEM((rows // SUB, wide, 3 * LANES), F32),
            pltpu.VMEM(block, F32),
            pltpu.VMEM(block, BF),
            pltpu.VMEM(block, BF),
        ]
        + [pltpu.VMEM((parts, size, groups * LANES), BF) for _, size in chunks]
        + [pltpu.VMEM((owners, 2, size, LANES), BF) for _, size in chunks] * 2
        + [pltpu.VMEM((owners, 3, size, LANES), BF) for _, size in chunks] * 2
        + [
            dma((4,)),
            dma((n,)),
            dma((2, groups // 4, 2)),
            dma((2, groups // 4, 2)),
            dma,
            dma,
            dma((n,)),
            dma((2,)),
            dma((2, n)),
            dma((2, n)),
        ],
        compiler_params=pltpu.CompilerParams(
            collective_id=0, has_side_effects=True, vmem_limit_bytes=48 * 1024 * 1024
        ),
    )(
        token_acts.reshape(slot_count * tok, hidden),
        out_grad.reshape(groups, parts, rows, width),
        counts.reshape(slot_count),
        params.reshape(block),
        first.reshape(block),
        second.reshape(block),
        old,
        rep,
        new,
    )
    return tuple(x.reshape(1, row_count, hidden) for x in out)


def solution(mesh):
    return jax.shard_map(
        functools.partial(local, mesh.shape["edp"], mesh.shape["ep"]),
        mesh=mesh,
        in_specs=(
            P("edp", "ep", None, None, None),
            P("edp", "ep", None, None),
            P("edp", "ep", None),
            P("ep", "edp", None),
            P("ep", "edp", None),
            P("ep", "edp", None),
            P(),
            P(),
            P(),
        ),
        out_specs=(P("ep", "edp", None), P("ep", "edp", None), P("ep", "edp", None)),
        check_vma=False,
    )
```

```python
import functools

import jax
import jax.numpy as jnp
from jax import lax
from jax.experimental import pallas as pl
from jax.experimental.pallas import tpu as pltpu
from jax.sharding import PartitionSpec as P

beta_one = 0.9
beta_two = 0.95
bias_one = 0.9999734386011124
bias_two = 0.994079470779666
decay_rate = 0.1
adam_eps = 1e-08

LANES = 128
SUB = 8
MESH = pl.DeviceIdType.MESH
BF = jnp.bfloat16
F32 = jnp.float32


def splits(rows):
    first = 32 if rows > 32 else rows
    return [(0, first)] + ([(first, rows - first)] if rows > first else [])


def kernel(groups, owners, *refs):
    (acts_ref, grad_ref, counts_ref, p_ref, f_ref, s_ref, old_ref, rep_ref, new_ref) = refs[:9]
    n_chunks = len(splits(p_ref.shape[1]))
    new_p = refs[9]
    oi = refs[10 : 10 + n_chunks]
    rest = list(refs[10 + n_chunks :])
    acts_all, p_v, f_v, s_v, p_st, p_in, p_out, m_in, pick, placed = rest[:10]
    rest = rest[10:]
    parts, rows, hidden = p_ref.shape
    cols = hidden // LANES
    tokens = acts_ref.shape[0]
    half = tokens // 2
    chunks = splits(rows)
    g_buf, gs, gi, os_ = (rest[i * n_chunks : (i + 1) * n_chunks] for i in range(4))
    rest = rest[4 * n_chunks :]
    (load_sem, g_sem, ring_send, ring_recv, pair_sem, rows_send, p_sem, m_sem, new_sem, gr_sem, out_sem) = rest

    r = lax.axis_index("edp")
    e = lax.axis_index("ep")
    chips = groups // 2
    core = lax.rem(r, 2)
    z = r // 2

    load_acts = pltpu.make_async_copy(acts_ref, acts_all.at[r], load_sem.at[0])
    load_p = pltpu.make_async_copy(p_ref, p_v, load_sem.at[1])
    load_f = pltpu.make_async_copy(f_ref, f_v, load_sem.at[2])
    load_s = pltpu.make_async_copy(s_ref, s_v, load_sem.at[3])
    load_acts.start()
    load_p.start()
    load_f.start()
    load_s.start()

    barrier = pltpu.get_barrier_semaphore()

    def greet_group(k, _):
        pl.semaphore_signal(
            barrier, inc=1, device_id=(lax.rem(r + k, groups), e), device_id_type=MESH
        )
        return 0

    def greet_owner(k, _):
        pl.semaphore_signal(
            barrier, inc=1, device_id=(r, lax.rem(e + k, owners)), device_id_type=MESH
        )
        return 0

    lax.fori_loop(1, owners, greet_owner, 0)
    lax.fori_loop(1, groups, greet_group, 0)

    load_acts.wait()
    token = lax.broadcasted_iota(jnp.int32, (half, hidden), 0)
    for slot in range(2):
        block = acts_all[r, slot * half : (slot + 1) * half, :].astype(F32)
        live = jnp.where(token < counts_ref[slot], block, 0.0)
        acts_all[r, slot * half : (slot + 1) * half, :] = live.astype(BF)
    load_p.wait()
    for q in range(parts):
        for c in range(cols):
            p_st[q * cols + c] = p_v[q, :, c * LANES : (c + 1) * LANES].astype(BF)
    load_f.wait()
    load_s.wait()

    pl.semaphore_wait(barrier, groups - 1 + owners - 1)

    def send_rows(i):
        first, size = chunks[i]
        lanes = pl.ds(pl.multiple_of(r * LANES, LANES), LANES)

        def body(k, _):
            to = lax.rem(r + k, groups)
            pltpu.make_async_remote_copy(
                src_ref=grad_ref.at[to, :, first : first + size, :],
                dst_ref=g_buf[i].at[:, :, lanes],
                send_sem=rows_send.at[i],
                recv_sem=g_sem.at[i],
                device_id=(to, e),
                device_id_type=MESH,
            ).start()
            return 0

        lax.fori_loop(1, groups, body, 0)
        pltpu.make_async_copy(
            grad_ref.at[r, :, first : first + size, :], g_buf[i].at[:, :, lanes], g_sem.at[i]
        ).start()

    def ring(direction, hop, h):
        away = hop if direction == 0 else chips - hop
        block = lax.rem(z + chips - away, chips) * 2 + core
        to = lax.rem(z + (1 if direction == 0 else chips - 1), chips) * 2 + core
        ref = acts_all.at[block, pl.ds(h * half, half), :]
        return pltpu.make_async_remote_copy(
            src_ref=ref,
            dst_ref=ref,
            send_sem=ring_send.at[direction, hop, h],
            recv_sem=ring_recv.at[direction, hop, h],
            device_id=(to, e),
            device_id_type=MESH,
        )

    def arrived(direction, hop, h):
        away = hop + 1 if direction == 0 else chips - hop - 1
        block = lax.rem(z + chips - away, chips) * 2 + core
        ref = acts_all.at[block, pl.ds(h * half, half), :]
        return ref, pltpu.make_async_copy(ref, ref, ring_recv.at[direction, hop, h])

    def to_pair(ref):
        pltpu.make_async_remote_copy(
            src_ref=ref,
            dst_ref=ref,
            send_sem=pair_sem.at[0],
            recv_sem=pair_sem.at[1],
            device_id=(r + 1 - 2 * core, e),
            device_id_type=MESH,
        ).start()

    far = chips // 2

    def goes(direction, hop, h):
        return hop < far - 1 or (hop == far - 1 and h == direction)

    ring_ops = [
        (direction, hop, h)
        for hop in range(far)
        for h in (0, 1)
        for direction in (0, 1)
        if goes(direction, hop, h)
    ]

    def spread(source, landing, sems):
        def body(k, _):
            to = lax.rem(e + k, owners)
            pltpu.make_async_remote_copy(
                src_ref=source(to),
                dst_ref=landing,
                send_sem=sems.at[0],
                recv_sem=sems.at[1],
                device_id=(r, to),
                device_id_type=MESH,
            ).start()
            return 0

        lax.fori_loop(1, owners, body, 0)
        pltpu.make_async_copy(source(e), landing, sems.at[1]).start()

    def block_of(ref):
        def at(j):
            lanes = pl.ds(pl.multiple_of(lax.rem(j, cols) * LANES, LANES), LANES)
            return ref.at[j // cols, :, lanes]

        return at

    def wait_all(ref, sem):
        pltpu.make_async_copy(ref, ref, sem).wait()

    for op in ring_ops:
        if op[1] == 0:
            ring(*op).start()
    spread(lambda j: p_st.at[j], p_in.at[e], p_sem)
    to_pair(acts_all.at[r])
    send_rows(0)
    spread(block_of(f_v), m_in.at[e, 0], m_sem)
    spread(block_of(s_v), m_in.at[e, 1], m_sem)

    wide = SUB * owners
    lane = lax.broadcasted_iota(jnp.int32, (SUB, wide), 1)
    sub = lax.broadcasted_iota(jnp.int32, (SUB, wide), 0)
    same_row = lax.rem(lane, SUB) == sub
    lane_expert = lane // SUB
    old_wide = jnp.zeros((SUB, wide), jnp.int32)
    rep_wide = jnp.zeros((SUB, wide), jnp.int32)
    for i in range(owners):
        old_wide = jnp.where(lane_expert == i, old_ref[i], old_wide)
        rep_wide = jnp.where(lane_expert == i, rep_ref[i], rep_wide)
    for d in range(owners):
        at = slice(d * SUB, (d + 1) * SUB)
        pick[at, :wide] = jnp.where(same_row & (old_wide == new_ref[d]), 1.0, 0.0)
        pick[at, wide:] = jnp.where(same_row & (rep_wide == new_ref[d]), 1.0, 0.0)

    def stack(block):
        return block.astype(F32).reshape(wide, LANES).astype(BF)

    def pass_on():
        wait_all(p_in, p_sem.at[1])
        move = pick[:, :wide].astype(BF)
        for t in range(rows // SUB):
            at = slice(t * SUB, (t + 1) * SUB)
            moved = jnp.dot(move, stack(p_in[:, at, :]), preferred_element_type=F32)
            p_out[:, at, :] = moved.reshape(owners, SUB, LANES).astype(BF)
        spread(lambda j: p_out.at[j], new_p.at[e], new_sem)

    for hop in range(far):
        for op in ring_ops:
            if op[1] != hop:
                continue
            direction, _, h = op
            ref, copy = arrived(*op)
            copy.wait()
            if hop + 1 < far and goes(direction, hop + 1, h):
                ring(direction, hop + 1, h).start()
            to_pair(ref)
        if hop == min(1, far - 1):
            pass_on()
        if hop == max(0, far - 2):
            for i in range(1, n_chunks):
                send_rows(i)
    for op in ring_ops:
        ring(*op).wait_send()
    mine = acts_all.at[pl.ds(0, chips)]
    wait_all(mine, pair_sem.at[1])

    def gradients(i):
        first, size = chunks[i]
        wait_all(g_buf[i], g_sem.at[i])
        width = groups * LANES
        block = g_buf[i][...].astype(F32).reshape(parts * size, width)
        in_own = lax.rem(lax.broadcasted_iota(jnp.int32, block.shape, 1), LANES) < LANES // 2
        left = jnp.concatenate(
            [jnp.where(in_own, block, 0.0).astype(BF), jnp.where(in_own, 0.0, block).astype(BF)], 0
        )
        for c0 in range(0, hidden, 256):
            n = min(256, hidden - c0)
            right = acts_all[:, :, c0 : c0 + n].reshape(groups * tokens, n)
            out = jnp.dot(left, right, preferred_element_type=F32)
            for slot in range(2):
                for q in range(parts):
                    at = (slot * parts + q) * size
                    for c in range(n // LANES):
                        piece = out[at : at + size, c * LANES : (c + 1) * LANES]
                        gs[i][q * cols + c0 // LANES + c, slot] = piece.astype(BF)
        spread(lambda j: gs[i].at[j], gi[i].at[e], gr_sem.at[i])

    def place():
        wait_all(m_in, m_sem.at[1])
        move = pick[:, :wide].astype(BF)
        for t in range(rows // SUB):
            at = slice(t * SUB, (t + 1) * SUB)
            both = jnp.concatenate([stack(m_in[:, item, at, :]) for item in range(2)], 1)
            placed[t] = jnp.dot(move, both, preferred_element_type=F32)

    def update(i):
        first, size = chunks[i]
        wait_all(gi[i], gr_sem.at[i, 1])
        both = pick[...].astype(BF)
        for t in range(size // SUB):
            at = slice(t * SUB, (t + 1) * SUB)
            terms = jnp.concatenate([stack(gi[i][:, item, at, :]) for item in range(2)], 0)
            gradient = jnp.dot(both, terms, preferred_element_type=F32)
            old = placed[first // SUB + t]
            first_old, second_old = old[:, :LANES], old[:, LANES:]
            first_new = beta_one * first_old + (1.0 - beta_one) * gradient
            second_new = beta_two * second_old + (1.0 - beta_two) * gradient * gradient
            for item, value in enumerate((first_new, second_new)):
                os_[i][:, item, at, :] = value.reshape(owners, SUB, LANES).astype(BF)
        spread(lambda j: os_[i].at[j], oi[i].at[e], out_sem.at[i])

    gradients(0)
    place()
    for i in range(1, n_chunks):
        gradients(i)
    for i in range(n_chunks):
        update(i)

    others = pl.ds(0, owners - 1)
    wait_all(mine, pair_sem.at[0])
    wait_all(p_st.at[others], p_sem.at[0])
    wait_all(m_in.at[others], m_sem.at[0])
    wait_all(p_out.at[others], new_sem.at[0])
    wait_all(new_p, new_sem.at[1])
    for i in range(n_chunks):
        wait_all(g_buf[i].at[:, :, pl.ds(0, (groups - 1) * LANES)], rows_send.at[i])
        wait_all(gs[i].at[others], gr_sem.at[i, 0])
        wait_all(os_[i].at[others], out_sem.at[i, 0])
        wait_all(oi[i], out_sem.at[i, 1])


def finish(chunks, p_ref, *refs):
    n = len(chunks)
    step_ref, first_ref, second_ref = refs[n:]
    for c in range(p_ref.shape[0]):
        lanes = slice(c * LANES, (c + 1) * LANES)
        for i, (first, size) in enumerate(chunks):
            at = slice(first, first + size)
            first_new, second_new = refs[i][c, 0], refs[i][c, 1]
            weights = p_ref[c, at, :].astype(F32)
            scaled = (first_new.astype(F32) / bias_one) / (
                jnp.sqrt(second_new.astype(F32) / bias_two) + adam_eps
            )
            step_ref[0, at, lanes] = -(scaled + decay_rate * weights)
            first_ref[0, at, lanes] = first_new
            second_ref[0, at, lanes] = second_new


def local(groups, owners, token_acts, out_grad, counts, params, first, second, old, rep, new):
    model_width, width = out_grad.shape[2:]
    slot_count, tok, hidden = token_acts.shape[2:]
    row_count = model_width // groups
    cols = hidden // LANES
    parts = owners // cols
    rows = row_count // parts
    chunks = splits(rows)
    block = (parts, rows, hidden)
    hbm = pl.BlockSpec(memory_space=pl.ANY)
    smem = pl.BlockSpec(memory_space=pltpu.SMEM)
    n = len(chunks)
    wide = SUB * owners
    dma = pltpu.SemaphoreType.DMA
    landed = pl.pallas_call(
        functools.partial(kernel, groups, owners),
        out_shape=[jax.ShapeDtypeStruct((owners, rows, LANES), BF)]
        + [jax.ShapeDtypeStruct((owners, 2, size, LANES), BF) for _, size in chunks],
        in_specs=[hbm, hbm, smem, hbm, hbm, hbm, smem, smem, smem],
        out_specs=[hbm] * (1 + n),
        scratch_shapes=[
            pltpu.VMEM((groups, slot_count * tok, hidden), BF),
            pltpu.VMEM(block, F32),
            pltpu.VMEM(block, BF),
            pltpu.VMEM(block, BF),
            pltpu.VMEM((owners, rows, LANES), BF),
            pltpu.VMEM((owners, rows, LANES), BF),
            pltpu.VMEM((owners, rows, LANES), BF),
            pltpu.VMEM((owners, 2, rows, LANES), BF),
            pltpu.VMEM((wide, 2 * wide), F32),
            pltpu.VMEM((rows // SUB, wide, 2 * LANES), F32),
        ]
        + [pltpu.VMEM((parts, size, groups * LANES), BF) for _, size in chunks]
        + [pltpu.VMEM((owners, 2, size, LANES), BF) for _, size in chunks] * 3
        + [
            dma((4,)),
            dma((n,)),
            dma((2, groups // 4, 2)),
            dma((2, groups // 4, 2)),
            dma((2,)),
            dma((n,)),
            dma((2,)),
            dma((2,)),
            dma((2,)),
            dma((n, 2)),
            dma((n, 2)),
        ],
        compiler_params=pltpu.CompilerParams(
            collective_id=0, has_side_effects=True, vmem_limit_bytes=60 * 1024 * 1024
        ),
    )(
        token_acts.reshape(slot_count * tok, hidden),
        out_grad.reshape(groups, parts, rows, width),
        counts.reshape(slot_count),
        params.reshape(block),
        first.reshape(block),
        second.reshape(block),
        old,
        rep,
        new,
    )
    out_block = pl.BlockSpec((1, rows, hidden), lambda q: (q, 0, 0))
    out = pl.pallas_call(
        functools.partial(finish, chunks),
        grid=(parts,),
        out_shape=[
            jax.ShapeDtypeStruct(block, F32),
            jax.ShapeDtypeStruct(block, BF),
            jax.ShapeDtypeStruct(block, BF),
        ],
        in_specs=[pl.BlockSpec((cols, rows, LANES), lambda q: (q, 0, 0))]
        + [pl.BlockSpec((cols, 2, size, LANES), lambda q: (q, 0, 0, 0)) for _, size in chunks],
        out_specs=[out_block] * 3,
    )(*landed)
    return tuple(x.reshape(1, row_count, hidden) for x in out)


def solution(mesh):
    return jax.shard_map(
        functools.partial(local, mesh.shape["edp"], mesh.shape["ep"]),
        mesh=mesh,
        in_specs=(
            P("edp", "ep", None, None, None),
            P("edp", "ep", None, None),
            P("edp", "ep", None),
            P("ep", "edp", None),
            P("ep", "edp", None),
            P("ep", "edp", None),
            P(),
            P(),
            P(),
        ),
        out_specs=(P("ep", "edp", None), P("ep", "edp", None), P("ep", "edp", None)),
        check_vma=False,
    )
```

```python
import functools

import jax
import jax.numpy as jnp
from jax import lax
from jax.experimental import pallas as pl
from jax.experimental.pallas import tpu as pltpu
from jax.sharding import PartitionSpec as P

beta_one = 0.9
beta_two = 0.95
bias_one = 0.9999734386011124
bias_two = 0.994079470779666
decay_rate = 0.1
adam_eps = 1e-08

LANES = 128
SUB = 8
MESH = pl.DeviceIdType.MESH
BF = jnp.bfloat16
F32 = jnp.float32


def splits(rows):
    first = rows // SUB * 3 // 7 * SUB
    return [(0, first), (first, rows - first)] if first else [(0, rows)]


def kernel(groups, owners, *refs):
    (acts_ref, grad_ref, counts_hbm, p_ref, f_ref, s_ref, old_hbm, rep_hbm, new_hbm) = refs[:9]
    n_chunks = len(splits(p_ref.shape[1]))
    new_p = refs[9]
    oi = refs[10 : 10 + n_chunks]
    rest = list(refs[10 + n_chunks :])
    counts_ref, old_ref, rep_ref, new_ref = rest[:4]
    acts_all, p_v, f_v, s_v, p_st, p_in, p_out, m_in, pick, placed = rest[4:14]
    rest = rest[14:]
    parts, rows, hidden = p_ref.shape
    cols = hidden // LANES
    tokens = acts_ref.shape[0]
    half = tokens // 2
    chunks = splits(rows)
    g_buf, gs, gi, os_ = (rest[i * n_chunks : (i + 1) * n_chunks] for i in range(4))
    rest = rest[4 * n_chunks :]
    (load_sem, g_sem, ring_send, ring_recv, pair_sem, rows_send, p_sem, m_sem, new_sem, gr_sem, out_sem) = rest

    r = lax.axis_index("edp")
    e = lax.axis_index("ep")
    chips = groups // 2
    core = lax.rem(r, 2)
    z = r // 2

    load_index = [
        pltpu.make_async_copy(a, b, load_sem.at[4 + k])
        for k, (a, b) in enumerate(
            ((counts_hbm, counts_ref), (old_hbm, old_ref), (rep_hbm, rep_ref), (new_hbm, new_ref))
        )
    ]
    load_acts = pltpu.make_async_copy(acts_ref, acts_all.at[r], load_sem.at[0])
    load_p = pltpu.make_async_copy(p_ref, p_v, load_sem.at[1])
    load_f = pltpu.make_async_copy(f_ref, f_v, load_sem.at[2])
    load_s = pltpu.make_async_copy(s_ref, s_v, load_sem.at[3])
    load_acts.start()
    for copy in load_index:
        copy.start()
    load_p.start()
    load_f.start()
    load_s.start()

    barrier = pltpu.get_barrier_semaphore()

    def greet_group(k, _):
        pl.semaphore_signal(
            barrier, inc=1, device_id=(lax.rem(r + k, groups), e), device_id_type=MESH
        )
        return 0

    def greet_owner(k, _):
        pl.semaphore_signal(
            barrier, inc=1, device_id=(r, lax.rem(e + k, owners)), device_id_type=MESH
        )
        return 0

    lax.fori_loop(1, owners, greet_owner, 0)
    lax.fori_loop(1, groups, greet_group, 0)

    load_acts.wait()
    for copy in load_index:
        copy.wait()
    token = lax.broadcasted_iota(jnp.int32, (half, hidden), 0)
    for slot in range(2):
        block = acts_all[r, slot * half : (slot + 1) * half, :].astype(F32)
        live = jnp.where(token < counts_ref[slot], block, 0.0)
        acts_all[r, slot * half : (slot + 1) * half, :] = live.astype(BF)
    load_p.wait()
    for q in range(parts):
        for c in range(cols):
            p_st[q * cols + c] = p_v[q, :, c * LANES : (c + 1) * LANES].astype(BF)
    load_f.wait()
    load_s.wait()

    pl.semaphore_wait(barrier, groups - 1 + owners - 1)

    def send_rows(i):
        first, size = chunks[i]
        lanes = pl.ds(pl.multiple_of(r * LANES, LANES), LANES)

        def body(k, _):
            to = lax.rem(r + k, groups)
            pltpu.make_async_remote_copy(
                src_ref=grad_ref.at[to, :, first : first + size, :],
                dst_ref=g_buf[i].at[:, :, lanes],
                send_sem=rows_send.at[i],
                recv_sem=g_sem.at[i],
                device_id=(to, e),
                device_id_type=MESH,
            ).start()
            return 0

        lax.fori_loop(1, groups, body, 0)
        pltpu.make_async_copy(
            grad_ref.at[r, :, first : first + size, :], g_buf[i].at[:, :, lanes], g_sem.at[i]
        ).start()

    def ring(direction, hop, h):
        away = hop if direction == 0 else chips - hop
        block = lax.rem(z + chips - away, chips) * 2 + core
        to = lax.rem(z + (1 if direction == 0 else chips - 1), chips) * 2 + core
        ref = acts_all.at[block, pl.ds(h * half, half), :]
        return pltpu.make_async_remote_copy(
            src_ref=ref,
            dst_ref=ref,
            send_sem=ring_send.at[direction, hop, h],
            recv_sem=ring_recv.at[direction, hop, h],
            device_id=(to, e),
            device_id_type=MESH,
        )

    def arrived(direction, hop, h):
        away = hop + 1 if direction == 0 else chips - hop - 1
        block = lax.rem(z + chips - away, chips) * 2 + core
        ref = acts_all.at[block, pl.ds(h * half, half), :]
        return ref, pltpu.make_async_copy(ref, ref, ring_recv.at[direction, hop, h])

    def to_pair(ref):
        pltpu.make_async_remote_copy(
            src_ref=ref,
            dst_ref=ref,
            send_sem=pair_sem.at[0],
            recv_sem=pair_sem.at[1],
            device_id=(r + 1 - 2 * core, e),
            device_id_type=MESH,
        ).start()

    far = chips // 2

    def goes(direction, hop, h):
        return hop < far - 1 or (hop == far - 1 and h == direction)

    ring_ops = [
        (direction, hop, h)
        for hop in range(far)
        for h in (0, 1)
        for direction in (0, 1)
        if goes(direction, hop, h)
    ]

    def spread(source, landing, sems):
        def body(k, _):
            to = lax.rem(e + k, owners)
            pltpu.make_async_remote_copy(
                src_ref=source(to),
                dst_ref=landing,
                send_sem=sems.at[0],
                recv_sem=sems.at[1],
                device_id=(r, to),
                device_id_type=MESH,
            ).start()
            return 0

        lax.fori_loop(1, owners, body, 0)
        pltpu.make_async_copy(source(e), landing, sems.at[1]).start()

    def block_of(ref):
        def at(j):
            lanes = pl.ds(pl.multiple_of(lax.rem(j, cols) * LANES, LANES), LANES)
            return ref.at[j // cols, :, lanes]

        return at

    def wait_all(ref, sem):
        pltpu.make_async_copy(ref, ref, sem).wait()

    for op in ring_ops:
        if op[1] == 0:
            ring(*op).start()
    spread(lambda j: p_st.at[j], p_in.at[e], p_sem)
    to_pair(acts_all.at[r])
    send_rows(0)
    spread(block_of(f_v), m_in.at[e, 0], m_sem)
    spread(block_of(s_v), m_in.at[e, 1], m_sem)

    wide = SUB * owners
    lane = lax.broadcasted_iota(jnp.int32, (SUB, wide), 1)
    sub = lax.broadcasted_iota(jnp.int32, (SUB, wide), 0)
    same_row = lax.rem(lane, SUB) == sub
    lane_expert = lane // SUB
    old_wide = jnp.zeros((SUB, wide), jnp.int32)
    rep_wide = jnp.zeros((SUB, wide), jnp.int32)
    for i in range(owners):
        old_wide = jnp.where(lane_expert == i, old_ref[i], old_wide)
        rep_wide = jnp.where(lane_expert == i, rep_ref[i], rep_wide)
    for d in range(owners):
        at = slice(d * SUB, (d + 1) * SUB)
        pick[at, :wide] = jnp.where(same_row & (old_wide == new_ref[d]), 1.0, 0.0)
        pick[at, wide:] = jnp.where(same_row & (rep_wide == new_ref[d]), 1.0, 0.0)

    def stack(block):
        return block.astype(F32).reshape(wide, LANES).astype(BF)

    def pass_on():
        wait_all(p_in, p_sem.at[1])
        move = pick[:, :wide].astype(BF)
        for t in range(rows // SUB):
            at = slice(t * SUB, (t + 1) * SUB)
            moved = jnp.dot(move, stack(p_in[:, at, :]), preferred_element_type=F32)
            p_out[:, at, :] = moved.reshape(owners, SUB, LANES).astype(BF)
        spread(lambda j: p_out.at[j], new_p.at[e], new_sem)

    for hop in range(far):
        for op in ring_ops:
            if op[1] != hop:
                continue
            direction, _, h = op
            ref, copy = arrived(*op)
            copy.wait()
            if hop + 1 < far and goes(direction, hop + 1, h):
                ring(direction, hop + 1, h).start()
            to_pair(ref)
        if hop == min(1, far - 1):
            pass_on()
        if hop == max(0, far - 2):
            for i in range(1, n_chunks):
                send_rows(i)
    for op in ring_ops:
        ring(*op).wait_send()
    mine = acts_all.at[pl.ds(0, chips)]
    wait_all(mine, pair_sem.at[1])

    def gradients(i):
        first, size = chunks[i]
        wait_all(g_buf[i], g_sem.at[i])
        width = groups * LANES
        block = g_buf[i][...].astype(F32).reshape(parts * size, width)
        in_own = lax.rem(lax.broadcasted_iota(jnp.int32, block.shape, 1), LANES) < LANES // 2
        left = jnp.concatenate(
            [jnp.where(in_own, block, 0.0).astype(BF), jnp.where(in_own, 0.0, block).astype(BF)], 0
        )
        for c0 in range(0, hidden, 256):
            n = min(256, hidden - c0)
            right = acts_all[:, :, c0 : c0 + n].reshape(groups * tokens, n)
            out = jnp.dot(left, right, preferred_element_type=F32)
            for slot in range(2):
                for q in range(parts):
                    at = (slot * parts + q) * size
                    for c in range(n // LANES):
                        piece = out[at : at + size, c * LANES : (c + 1) * LANES]
                        gs[i][q * cols + c0 // LANES + c, slot] = piece.astype(BF)
        spread(lambda j: gs[i].at[j], gi[i].at[e], gr_sem.at[i])

    def place():
        wait_all(m_in, m_sem.at[1])
        move = pick[:, :wide].astype(BF)
        for t in range(rows // SUB):
            at = slice(t * SUB, (t + 1) * SUB)
            both = jnp.concatenate([stack(m_in[:, item, at, :]) for item in range(2)], 1)
            placed[t] = jnp.dot(move, both, preferred_element_type=F32)

    def update(i):
        first, size = chunks[i]
        wait_all(gi[i], gr_sem.at[i, 1])
        both = pick[...].astype(BF)
        for t in range(size // SUB):
            at = slice(t * SUB, (t + 1) * SUB)
            terms = jnp.concatenate([stack(gi[i][:, item, at, :]) for item in range(2)], 0)
            gradient = jnp.dot(both, terms, preferred_element_type=F32)
            old = placed[first // SUB + t]
            first_old, second_old = old[:, :LANES], old[:, LANES:]
            first_new = beta_one * first_old + (1.0 - beta_one) * gradient
            second_new = beta_two * second_old + (1.0 - beta_two) * gradient * gradient
            for item, value in enumerate((first_new, second_new)):
                os_[i][:, item, at, :] = value.reshape(owners, SUB, LANES).astype(BF)
        spread(lambda j: os_[i].at[j], oi[i].at[e], out_sem.at[i])

    gradients(0)
    place()
    for i in range(1, n_chunks):
        gradients(i)
    for i in range(n_chunks):
        update(i)

    others = pl.ds(0, owners - 1)
    wait_all(mine, pair_sem.at[0])
    wait_all(p_st.at[others], p_sem.at[0])
    wait_all(m_in.at[others], m_sem.at[0])
    wait_all(p_out.at[others], new_sem.at[0])
    wait_all(new_p, new_sem.at[1])
    for i in range(n_chunks):
        wait_all(g_buf[i].at[:, :, pl.ds(0, (groups - 1) * LANES)], rows_send.at[i])
        wait_all(gs[i].at[others], gr_sem.at[i, 0])
        wait_all(os_[i].at[others], out_sem.at[i, 0])
        wait_all(oi[i], out_sem.at[i, 1])


def finish(chunks, p_ref, *refs):
    n = len(chunks)
    step_ref, first_ref, second_ref, step_v, first_v, second_v, sems = refs[n:]
    parts, _, hidden = step_v.shape
    cols = hidden // LANES
    copies = []
    for q in range(parts):
        for c in range(cols):
            lanes = slice(c * LANES, (c + 1) * LANES)
            for i, (first, size) in enumerate(chunks):
                at = slice(first, first + size)
                first_new, second_new = refs[i][q * cols + c, 0], refs[i][q * cols + c, 1]
                weights = p_ref[q * cols + c, at, :].astype(F32)
                root = jnp.sqrt(second_new.astype(F32) * (bias_one * bias_one / bias_two))
                scaled = first_new.astype(F32) / (root + bias_one * adam_eps)
                step_v[q, at, lanes] = -(scaled + decay_rate * weights)
                first_v[q, at, lanes] = first_new
                second_v[q, at, lanes] = second_new
        for k, (a, b) in enumerate(
            ((step_v, step_ref), (first_v, first_ref), (second_v, second_ref))
        ):
            copies.append(pltpu.make_async_copy(a.at[q], b.at[q], sems.at[k, q]))
            copies[-1].start()
    for copy in copies:
        copy.wait()


def local(groups, owners, token_acts, out_grad, counts, params, first, second, old, rep, new):
    model_width, width = out_grad.shape[2:]
    slot_count, tok, hidden = token_acts.shape[2:]
    row_count = model_width // groups
    cols = hidden // LANES
    parts = owners // cols
    rows = row_count // parts
    chunks = splits(rows)
    block = (parts, rows, hidden)
    hbm = pl.BlockSpec(memory_space=pltpu.HBM)
    vmem = pl.BlockSpec(memory_space=pltpu.VMEM)
    n = len(chunks)
    wide = SUB * owners
    dma = pltpu.SemaphoreType.DMA
    operands = (
        token_acts.reshape(slot_count * tok, hidden),
        out_grad.reshape(groups, parts, rows, width),
        counts.reshape(slot_count),
        params.reshape(block),
        first.reshape(block),
        second.reshape(block),
        old,
        rep,
        new,
    )
    landed = pl.pallas_call(
        functools.partial(kernel, groups, owners),
        out_shape=[jax.ShapeDtypeStruct((owners, rows, LANES), BF)]
        + [jax.ShapeDtypeStruct((owners, 2, size, LANES), BF) for _, size in chunks],
        in_specs=[hbm] * len(operands),
        out_specs=[vmem] * (1 + n),
        scratch_shapes=[
            pltpu.SMEM((slot_count,), jnp.int32),
            pltpu.SMEM((owners,), jnp.int32),
            pltpu.SMEM((owners,), jnp.int32),
            pltpu.SMEM((owners,), jnp.int32),
            pltpu.VMEM((groups, slot_count * tok, hidden), BF),
            pltpu.VMEM(block, F32),
            pltpu.VMEM(block, BF),
            pltpu.VMEM(block, BF),
            pltpu.VMEM((owners, rows, LANES), BF),
            pltpu.VMEM((owners, rows, LANES), BF),
            pltpu.VMEM((owners, rows, LANES), BF),
            pltpu.VMEM((owners, 2, rows, LANES), BF),
            pltpu.VMEM((wide, 2 * wide), F32),
            pltpu.VMEM((rows // SUB, wide, 2 * LANES), F32),
        ]
        + [pltpu.VMEM((parts, size, groups * LANES), BF) for _, size in chunks]
        + [pltpu.VMEM((owners, 2, size, LANES), BF) for _, size in chunks] * 3
        + [
            dma((8,)),
            dma((n,)),
            dma((2, groups // 4, 2)),
            dma((2, groups // 4, 2)),
            dma((2,)),
            dma((n,)),
            dma((2,)),
            dma((2,)),
            dma((2,)),
            dma((n, 2)),
            dma((n, 2)),
        ],
        compiler_params=pltpu.CompilerParams(
            collective_id=0, has_side_effects=True, vmem_limit_bytes=36 * 1024 * 1024
        ),
    )(
        *(pltpu.with_memory_space_constraint(v, pltpu.HBM) for v in operands)
    )
    out = pl.pallas_call(
        functools.partial(finish, chunks),
        out_shape=[
            jax.ShapeDtypeStruct(block, F32),
            jax.ShapeDtypeStruct(block, BF),
            jax.ShapeDtypeStruct(block, BF),
        ],
        in_specs=[vmem] * (1 + n),
        out_specs=[pl.BlockSpec(memory_space=pltpu.HBM)] * 3,
        scratch_shapes=[
            pltpu.VMEM(block, F32),
            pltpu.VMEM(block, BF),
            pltpu.VMEM(block, BF),
            dma((3, parts)),
        ],
        compiler_params=pltpu.CompilerParams(vmem_limit_bytes=16 * 1024 * 1024),
    )(*landed)
    return tuple(x.reshape(1, row_count, hidden) for x in out)


def solution(mesh):
    return jax.shard_map(
        functools.partial(local, mesh.shape["edp"], mesh.shape["ep"]),
        mesh=mesh,
        in_specs=(
            P("edp", "ep", None, None, None),
            P("edp", "ep", None, None),
            P("edp", "ep", None),
            P("ep", "edp", None),
            P("ep", "edp", None),
            P("ep", "edp", None),
            P(),
            P(),
            P(),
        ),
        out_specs=(P("ep", "edp", None), P("ep", "edp", None), P("ep", "edp", None)),
        check_vma=False,
    )
```

```python
import functools

import jax
import jax.numpy as jnp
from jax import lax
from jax.experimental import pallas as pl
from jax.experimental.pallas import tpu as pltpu
from jax.sharding import PartitionSpec as P

beta_one = 0.9
beta_two = 0.95
bias_one = 0.9999734386011124
bias_two = 0.994079470779666
decay_rate = 0.1
adam_eps = 1e-08

LANES = 128
SUB = 8
MESH = pl.DeviceIdType.MESH
BF = jnp.bfloat16
F32 = jnp.float32


def splits(rows):
    first = rows // SUB * 3 // 7 * SUB
    return [(0, first), (first, rows - first)] if first else [(0, rows)]


def finish_part(chunk, q, cols, p_ref, moments_ref, results, row):
    first, size = chunk
    step, first_out, second_out = results
    at = slice(row, row + size)
    for c in range(cols):
        lanes = slice(c * LANES, (c + 1) * LANES)
        first_new, second_new = moments_ref[q * cols + c, 0], moments_ref[q * cols + c, 1]
        weights = p_ref[q * cols + c, first : first + size, :].astype(F32)
        root = jnp.sqrt(second_new.astype(F32) * (bias_one * bias_one / bias_two))
        scaled = first_new.astype(F32) / (root + bias_one * adam_eps)
        step[q, at, lanes] = -(scaled + decay_rate * weights)
        first_out[q, at, lanes] = first_new
        second_out[q, at, lanes] = second_new


def kernel(groups, owners, *refs):
    (acts_ref, grad_ref, counts_hbm, p_ref, f_ref, s_ref, old_hbm, rep_hbm, new_hbm) = refs[:9]
    n_chunks = len(splits(p_ref.shape[1]))
    new_p = refs[9]
    results = refs[11:14]
    rest = list(refs[14:])
    counts_ref, old_ref, rep_ref, new_ref = rest[:4]
    acts_all, p_v, f_v, s_v, p_st, p_in, p_out, m_in, pick, placed = rest[4:14]
    rest = rest[14:]
    parts, rows, hidden = p_ref.shape
    cols = hidden // LANES
    tokens = acts_ref.shape[0]
    half = tokens // 2
    chunks = splits(rows)
    g_buf, gs, gi, os_ = (rest[i * n_chunks : (i + 1) * n_chunks] for i in range(4))
    oi = rest[4 * n_chunks : 5 * n_chunks - 1] + [refs[10]]
    rest = rest[5 * n_chunks - 1 :]
    (load_sem, g_sem, ring_send, ring_recv, pair_sem, rows_send, p_sem, m_sem, new_sem, gr_sem, out_sem) = rest

    r = lax.axis_index("edp")
    e = lax.axis_index("ep")
    chips = groups // 2
    core = lax.rem(r, 2)
    z = r // 2

    barrier = pltpu.get_barrier_semaphore()

    def greet_group(k, _):
        pl.semaphore_signal(
            barrier, inc=1, device_id=(lax.rem(r + k, groups), e), device_id_type=MESH
        )
        return 0

    def greet_owner(k, _):
        pl.semaphore_signal(
            barrier, inc=1, device_id=(r, lax.rem(e + k, owners)), device_id_type=MESH
        )
        return 0

    lax.fori_loop(1, owners, greet_owner, 0)
    lax.fori_loop(1, groups, greet_group, 0)

    load_index = [
        pltpu.make_async_copy(a, b, load_sem.at[4 + k])
        for k, (a, b) in enumerate(
            ((counts_hbm, counts_ref), (old_hbm, old_ref), (rep_hbm, rep_ref), (new_hbm, new_ref))
        )
    ]
    load_acts = pltpu.make_async_copy(acts_ref, acts_all.at[r], load_sem.at[0])
    load_p = pltpu.make_async_copy(p_ref, p_v, load_sem.at[1])
    load_f = pltpu.make_async_copy(f_ref, f_v, load_sem.at[2])
    load_s = pltpu.make_async_copy(s_ref, s_v, load_sem.at[3])
    load_acts.start()
    for copy in load_index:
        copy.start()
    load_p.start()
    load_f.start()
    load_s.start()

    load_acts.wait()
    for copy in load_index:
        copy.wait()
    token = lax.broadcasted_iota(jnp.int32, (half, hidden), 0)
    for slot in range(2):
        block = acts_all[r, slot * half : (slot + 1) * half, :].astype(F32)
        live = jnp.where(token < counts_ref[slot], block, 0.0)
        acts_all[r, slot * half : (slot + 1) * half, :] = live.astype(BF)
    load_p.wait()
    for q in range(parts):
        for c in range(cols):
            p_st[q * cols + c] = p_v[q, :, c * LANES : (c + 1) * LANES].astype(BF)
    load_f.wait()
    load_s.wait()

    pl.semaphore_wait(barrier, groups - 1 + owners - 1)

    def send_rows(i):
        first, size = chunks[i]
        lanes = pl.ds(pl.multiple_of(r * LANES, LANES), LANES)

        def body(k, _):
            to = lax.rem(r + k, groups)
            pltpu.make_async_remote_copy(
                src_ref=grad_ref.at[to, :, first : first + size, :],
                dst_ref=g_buf[i].at[:, :, lanes],
                send_sem=rows_send.at[i],
                recv_sem=g_sem.at[i],
                device_id=(to, e),
                device_id_type=MESH,
            ).start()
            return 0

        lax.fori_loop(1, groups, body, 0)
        pltpu.make_async_copy(
            grad_ref.at[r, :, first : first + size, :], g_buf[i].at[:, :, lanes], g_sem.at[i]
        ).start()

    def ring(direction, hop, h):
        away = hop if direction == 0 else chips - hop
        block = lax.rem(z + chips - away, chips) * 2 + core
        to = lax.rem(z + (1 if direction == 0 else chips - 1), chips) * 2 + core
        ref = acts_all.at[block, pl.ds(h * half, half), :]
        return pltpu.make_async_remote_copy(
            src_ref=ref,
            dst_ref=ref,
            send_sem=ring_send.at[direction, hop, h],
            recv_sem=ring_recv.at[direction, hop, h],
            device_id=(to, e),
            device_id_type=MESH,
        )

    def arrived(direction, hop, h):
        away = hop + 1 if direction == 0 else chips - hop - 1
        block = lax.rem(z + chips - away, chips) * 2 + core
        ref = acts_all.at[block, pl.ds(h * half, half), :]
        return ref, pltpu.make_async_copy(ref, ref, ring_recv.at[direction, hop, h])

    def to_pair(ref):
        pltpu.make_async_remote_copy(
            src_ref=ref,
            dst_ref=ref,
            send_sem=pair_sem.at[0],
            recv_sem=pair_sem.at[1],
            device_id=(r + 1 - 2 * core, e),
            device_id_type=MESH,
        ).start()

    far = chips // 2

    def goes(direction, hop, h):
        return hop < far - 1 or (hop == far - 1 and h == direction)

    ring_ops = [
        (direction, hop, h)
        for hop in range(far)
        for h in (0, 1)
        for direction in (0, 1)
        if goes(direction, hop, h)
    ]

    def spread(source, landing, sems):
        def body(k, _):
            to = lax.rem(e + k, owners)
            pltpu.make_async_remote_copy(
                src_ref=source(to),
                dst_ref=landing,
                send_sem=sems.at[0],
                recv_sem=sems.at[1],
                device_id=(r, to),
                device_id_type=MESH,
            ).start()
            return 0

        lax.fori_loop(1, owners, body, 0)
        pltpu.make_async_copy(source(e), landing, sems.at[1]).start()

    def block_of(ref):
        def at(j):
            lanes = pl.ds(pl.multiple_of(lax.rem(j, cols) * LANES, LANES), LANES)
            return ref.at[j // cols, :, lanes]

        return at

    def wait_all(ref, sem):
        pltpu.make_async_copy(ref, ref, sem).wait()

    spread(lambda j: p_st.at[j], p_in.at[e], p_sem)
    for op in ring_ops:
        if op[1] == 0:
            ring(*op).start()
    to_pair(acts_all.at[r])
    send_rows(0)
    spread(block_of(f_v), m_in.at[e, 0], m_sem)
    spread(block_of(s_v), m_in.at[e, 1], m_sem)

    wide = SUB * owners
    lane = lax.broadcasted_iota(jnp.int32, (SUB, wide), 1)
    sub = lax.broadcasted_iota(jnp.int32, (SUB, wide), 0)
    same_row = lax.rem(lane, SUB) == sub
    lane_expert = lane // SUB
    old_wide = jnp.zeros((SUB, wide), jnp.int32)
    rep_wide = jnp.zeros((SUB, wide), jnp.int32)
    for i in range(owners):
        old_wide = jnp.where(lane_expert == i, old_ref[i], old_wide)
        rep_wide = jnp.where(lane_expert == i, rep_ref[i], rep_wide)
    for d in range(owners):
        at = slice(d * SUB, (d + 1) * SUB)
        pick[at, :wide] = jnp.where(same_row & (old_wide == new_ref[d]), 1.0, 0.0)
        pick[at, wide:] = jnp.where(same_row & (rep_wide == new_ref[d]), 1.0, 0.0)

    def stack(block):
        return block.astype(F32).reshape(wide, LANES).astype(BF)

    def pass_on():
        wait_all(p_in, p_sem.at[1])
        move = pick[:, :wide].astype(BF)
        for t in range(rows // SUB):
            at = slice(t * SUB, (t + 1) * SUB)
            moved = jnp.dot(move, stack(p_in[:, at, :]), preferred_element_type=F32)
            p_out[:, at, :] = moved.reshape(owners, SUB, LANES).astype(BF)
        spread(lambda j: p_out.at[j], new_p.at[e], new_sem)

    for hop in range(far):
        for op in ring_ops:
            if op[1] != hop:
                continue
            direction, _, h = op
            ref, copy = arrived(*op)
            copy.wait()
            if hop + 1 < far and goes(direction, hop + 1, h):
                ring(direction, hop + 1, h).start()
            to_pair(ref)
        if hop == min(1, far - 1):
            pass_on()
        if hop == max(0, far - 2):
            for i in range(1, n_chunks):
                send_rows(i)
    for op in ring_ops:
        ring(*op).wait_send()
    mine = acts_all.at[pl.ds(0, chips)]
    wait_all(mine, pair_sem.at[1])

    def gradients(i):
        first, size = chunks[i]
        wait_all(g_buf[i], g_sem.at[i])
        width = groups * LANES
        block = g_buf[i][...].astype(F32).reshape(parts * size, width)
        in_own = lax.rem(lax.broadcasted_iota(jnp.int32, block.shape, 1), LANES) < LANES // 2
        left = jnp.concatenate(
            [jnp.where(in_own, block, 0.0).astype(BF), jnp.where(in_own, 0.0, block).astype(BF)], 0
        )
        for c0 in range(0, hidden, 256):
            n = min(256, hidden - c0)
            right = acts_all[:, :, c0 : c0 + n].reshape(groups * tokens, n)
            out = jnp.dot(left, right, preferred_element_type=F32)
            for slot in range(2):
                for q in range(parts):
                    at = (slot * parts + q) * size
                    for c in range(n // LANES):
                        piece = out[at : at + size, c * LANES : (c + 1) * LANES]
                        gs[i][q * cols + c0 // LANES + c, slot] = piece.astype(BF)
        spread(lambda j: gs[i].at[j], gi[i].at[e], gr_sem.at[i])

    def place():
        wait_all(m_in, m_sem.at[1])
        move = pick[:, :wide].astype(BF)
        for t in range(rows // SUB):
            at = slice(t * SUB, (t + 1) * SUB)
            both = jnp.concatenate([stack(m_in[:, item, at, :]) for item in range(2)], 1)
            placed[t] = jnp.dot(move, both, preferred_element_type=F32)

    def update(i):
        first, size = chunks[i]
        wait_all(gi[i], gr_sem.at[i, 1])
        both = pick[...].astype(BF)
        for t in range(size // SUB):
            at = slice(t * SUB, (t + 1) * SUB)
            terms = jnp.concatenate([stack(gi[i][:, item, at, :]) for item in range(2)], 0)
            gradient = jnp.dot(both, terms, preferred_element_type=F32)
            old = placed[first // SUB + t]
            first_old, second_old = old[:, :LANES], old[:, LANES:]
            first_new = beta_one * first_old + (1.0 - beta_one) * gradient
            second_new = beta_two * second_old + (1.0 - beta_two) * gradient * gradient
            for item, value in enumerate((first_new, second_new)):
                os_[i][:, item, at, :] = value.reshape(owners, SUB, LANES).astype(BF)
        spread(lambda j: os_[i].at[j], oi[i].at[e], out_sem.at[i])

    gradients(0)
    place()
    for i in range(1, n_chunks):
        gradients(i)
    for i in range(n_chunks):
        update(i)

    wait_all(new_p, new_sem.at[1])
    for i in range(n_chunks - 1):
        wait_all(oi[i], out_sem.at[i, 1])
        for q in range(parts):
            finish_part(chunks[i], q, cols, new_p, oi[i], results, chunks[i][0])

    others = pl.ds(0, owners - 1)
    wait_all(mine, pair_sem.at[0])
    wait_all(p_st.at[others], p_sem.at[0])
    wait_all(m_in.at[others], m_sem.at[0])
    wait_all(p_out.at[others], new_sem.at[0])
    for i in range(n_chunks):
        wait_all(g_buf[i].at[:, :, pl.ds(0, (groups - 1) * LANES)], rows_send.at[i])
        wait_all(gs[i].at[others], gr_sem.at[i, 0])
        wait_all(os_[i].at[others], out_sem.at[i, 0])
    wait_all(oi[n_chunks - 1], out_sem.at[n_chunks - 1, 1])


def finish(chunk, p_ref, moments_ref, *refs):
    done, outs, last, sems = refs[:3], refs[3:6], refs[6:9], refs[9]
    first, size = chunk
    parts, _, hidden = done[0].shape
    copies = []

    def copy(k, q, source, rows):
        target = outs[k].at[:, rows, :] if q == parts else outs[k].at[q, rows, :]
        copies.append(pltpu.make_async_copy(source, target, sems.at[k, q]))
        copies[-1].start()

    if first:
        for k in range(3):
            copy(k, parts, done[k].at[:, pl.ds(0, first), :], pl.ds(0, first))
    for q in range(parts):
        finish_part(chunk, q, hidden // LANES, p_ref, moments_ref, last, 0)
        for k in range(3):
            copy(k, q, last[k].at[q], pl.ds(first, size))
    for started in copies:
        started.wait()


def local(groups, owners, token_acts, out_grad, counts, params, first, second, old, rep, new):
    model_width, width = out_grad.shape[2:]
    slot_count, tok, hidden = token_acts.shape[2:]
    row_count = model_width // groups
    cols = hidden // LANES
    parts = owners // cols
    rows = row_count // parts
    chunks = splits(rows)
    block = (parts, rows, hidden)
    hbm = pl.BlockSpec(memory_space=pltpu.HBM)
    vmem = pl.BlockSpec(memory_space=pltpu.VMEM)
    n = len(chunks)
    wide = SUB * owners
    dma = pltpu.SemaphoreType.DMA
    operands = (
        token_acts.reshape(slot_count * tok, hidden),
        out_grad.reshape(groups, parts, rows, width),
        counts.reshape(slot_count),
        params.reshape(block),
        first.reshape(block),
        second.reshape(block),
        old,
        rep,
        new,
    )
    landed = pl.pallas_call(
        functools.partial(kernel, groups, owners),
        out_shape=[jax.ShapeDtypeStruct((owners, rows, LANES), BF)]
        + [jax.ShapeDtypeStruct((owners, 2, chunks[-1][1], LANES), BF)]
        + [jax.ShapeDtypeStruct(block, kind) for kind in (F32, BF, BF)],
        in_specs=[hbm] * len(operands),
        out_specs=[vmem] * 5,
        scratch_shapes=[
            pltpu.SMEM((slot_count,), jnp.int32),
            pltpu.SMEM((owners,), jnp.int32),
            pltpu.SMEM((owners,), jnp.int32),
            pltpu.SMEM((owners,), jnp.int32),
            pltpu.VMEM((groups, slot_count * tok, hidden), BF),
            pltpu.VMEM(block, F32),
            pltpu.VMEM(block, BF),
            pltpu.VMEM(block, BF),
            pltpu.VMEM((owners, rows, LANES), BF),
            pltpu.VMEM((owners, rows, LANES), BF),
            pltpu.VMEM((owners, rows, LANES), BF),
            pltpu.VMEM((owners, 2, rows, LANES), BF),
            pltpu.VMEM((wide, 2 * wide), F32),
            pltpu.VMEM((rows // SUB, wide, 2 * LANES), F32),
        ]
        + [pltpu.VMEM((parts, size, groups * LANES), BF) for _, size in chunks]
        + [pltpu.VMEM((owners, 2, size, LANES), BF) for _, size in chunks] * 3
        + [pltpu.VMEM((owners, 2, size, LANES), BF) for _, size in chunks[:-1]]
        + [
            dma((8,)),
            dma((n,)),
            dma((2, groups // 4, 2)),
            dma((2, groups // 4, 2)),
            dma((2,)),
            dma((n,)),
            dma((2,)),
            dma((2,)),
            dma((2,)),
            dma((n, 2)),
            dma((n, 2)),
        ],
        compiler_params=pltpu.CompilerParams(
            collective_id=0, has_side_effects=True, vmem_limit_bytes=36 * 1024 * 1024
        ),
    )(
        *(pltpu.with_memory_space_constraint(v, pltpu.HBM) for v in operands)
    )
    last = (parts, chunks[-1][1], hidden)
    out = pl.pallas_call(
        functools.partial(finish, chunks[-1]),
        out_shape=[jax.ShapeDtypeStruct(block, kind) for kind in (F32, BF, BF)],
        in_specs=[vmem] * 5,
        out_specs=[hbm] * 3,
        scratch_shapes=[pltpu.VMEM(last, kind) for kind in (F32, BF, BF)] + [dma((3, parts + 1))],
        compiler_params=pltpu.CompilerParams(vmem_limit_bytes=16 * 1024 * 1024),
    )(*landed)
    return tuple(x.reshape(1, row_count, hidden) for x in out)


def solution(mesh):
    return jax.shard_map(
        functools.partial(local, mesh.shape["edp"], mesh.shape["ep"]),
        mesh=mesh,
        in_specs=(
            P("edp", "ep", None, None, None),
            P("edp", "ep", None, None),
            P("edp", "ep", None),
            P("ep", "edp", None),
            P("ep", "edp", None),
            P("ep", "edp", None),
            P(),
            P(),
            P(),
        ),
        out_specs=(P("ep", "edp", None), P("ep", "edp", None), P("ep", "edp", None)),
        check_vma=False,
    )
```

```python
import functools

import jax
import jax.numpy as jnp
from jax import lax
from jax.experimental import pallas as pl
from jax.experimental.pallas import tpu as pltpu
from jax.sharding import PartitionSpec as P

beta_one = 0.9
beta_two = 0.95
bias_one = 0.9999734386011124
bias_two = 0.994079470779666
decay_rate = 0.1
adam_eps = 1e-08

LANES = 128
SUB = 8
MESH = pl.DeviceIdType.MESH
BF = jnp.bfloat16
F32 = jnp.float32


def splits(rows):
    first = rows // SUB * 3 // 7 * SUB
    return [(0, first), (first, rows - first)] if first else [(0, rows)]


def finish_part(chunk, q, cols, p_ref, moments_ref, results, row):
    first, size = chunk
    step, first_out, second_out = results
    at = slice(row, row + size)
    for c in range(cols):
        lanes = slice(c * LANES, (c + 1) * LANES)
        first_new, second_new = moments_ref[q * cols + c, 0], moments_ref[q * cols + c, 1]
        weights = p_ref[q * cols + c, first : first + size, :].astype(F32)
        root = jnp.sqrt(second_new.astype(F32) * (bias_one * bias_one / bias_two))
        scaled = first_new.astype(F32) / (root + bias_one * adam_eps)
        step[q, at, lanes] = -(scaled + decay_rate * weights)
        first_out[q, at, lanes] = first_new
        second_out[q, at, lanes] = second_new


def kernel(groups, owners, *refs):
    (acts_ref, grad_ref, counts_hbm, p_ref, f_ref, s_ref, old_hbm, rep_hbm, new_hbm) = refs[:9]
    n_chunks = len(splits(p_ref.shape[1]))
    new_p = refs[9]
    results = refs[11:14]
    rest = list(refs[14:])
    counts_ref, old_ref, rep_ref, new_ref = rest[:4]
    acts_all, p_v, f_v, s_v, p_st, p_in, p_out, m_in, m_st, pick, placed = rest[4:15]
    rest = rest[15:]
    parts, rows, hidden = p_ref.shape
    cols = hidden // LANES
    tokens = acts_ref.shape[0]
    half = tokens // 2
    chunks = splits(rows)
    g_buf, gs, gi, os_ = (rest[i * n_chunks : (i + 1) * n_chunks] for i in range(4))
    oi = rest[4 * n_chunks : 5 * n_chunks - 1] + [refs[10]]
    rest = rest[5 * n_chunks - 1 :]
    (load_sem, g_sem, ring_send, ring_recv, pair_sem, rows_send, p_sem, m_sem, new_sem, gr_sem, out_sem) = rest

    r = lax.axis_index("edp")
    e = lax.axis_index("ep")
    chips = groups // 2
    core = lax.rem(r, 2)
    z = r // 2

    barrier = pltpu.get_barrier_semaphore()

    def greet_group(k, _):
        pl.semaphore_signal(
            barrier, inc=1, device_id=(lax.rem(r + k, groups), e), device_id_type=MESH
        )
        return 0

    def greet_owner(k, _):
        pl.semaphore_signal(
            barrier, inc=1, device_id=(r, lax.rem(e + k, owners)), device_id_type=MESH
        )
        return 0

    for k in range(1, owners):
        greet_owner(k, 0)
    for k in range(1, groups):
        greet_group(k, 0)

    load_index = [
        pltpu.make_async_copy(a, b, load_sem.at[4 + k])
        for k, (a, b) in enumerate(
            ((counts_hbm, counts_ref), (old_hbm, old_ref), (rep_hbm, rep_ref), (new_hbm, new_ref))
        )
    ]
    load_acts = pltpu.make_async_copy(acts_ref, acts_all.at[r], load_sem.at[0])
    load_p = pltpu.make_async_copy(p_ref, p_v, load_sem.at[1])
    load_f = pltpu.make_async_copy(f_ref, f_v, load_sem.at[2])
    load_s = pltpu.make_async_copy(s_ref, s_v, load_sem.at[3])
    load_acts.start()
    for copy in load_index:
        copy.start()
    load_p.start()
    load_f.start()
    load_s.start()

    load_acts.wait()
    for copy in load_index:
        copy.wait()
    token = lax.broadcasted_iota(jnp.int32, (half, hidden), 0)
    for slot in range(2):
        block = acts_all[r, slot * half : (slot + 1) * half, :].astype(F32)
        live = jnp.where(token < counts_ref[slot], block, 0.0)
        acts_all[r, slot * half : (slot + 1) * half, :] = live.astype(BF)
    load_p.wait()
    for q in range(parts):
        for c in range(cols):
            p_st[q * cols + c] = p_v[q, :, c * LANES : (c + 1) * LANES].astype(BF)
    load_f.wait()
    load_s.wait()
    for q in range(parts):
        for c in range(cols):
            lanes = slice(c * LANES, (c + 1) * LANES)
            m_st[q * cols + c, 0] = f_v[q, :, lanes]
            m_st[q * cols + c, 1] = s_v[q, :, lanes]

    pl.semaphore_wait(barrier, groups - 1 + owners - 1)

    def send_rows(i):
        first, size = chunks[i]
        lanes = pl.ds(pl.multiple_of(r * LANES, LANES), LANES)

        def body(k, _):
            to = lax.rem(r + k, groups)
            pltpu.make_async_remote_copy(
                src_ref=grad_ref.at[to, :, first : first + size, :],
                dst_ref=g_buf[i].at[:, :, lanes],
                send_sem=rows_send.at[i],
                recv_sem=g_sem.at[i],
                device_id=(to, e),
                device_id_type=MESH,
            ).start()
            return 0

        lax.fori_loop(1, groups, body, 0)
        pltpu.make_async_copy(
            grad_ref.at[r, :, first : first + size, :], g_buf[i].at[:, :, lanes], g_sem.at[i]
        ).start()

    def ring(direction, hop, h):
        away = hop if direction == 0 else chips - hop
        block = lax.rem(z + chips - away, chips) * 2 + core
        to = lax.rem(z + (1 if direction == 0 else chips - 1), chips) * 2 + core
        ref = acts_all.at[block, pl.ds(h * half, half), :]
        return pltpu.make_async_remote_copy(
            src_ref=ref,
            dst_ref=ref,
            send_sem=ring_send.at[direction, hop, h],
            recv_sem=ring_recv.at[direction, hop, h],
            device_id=(to, e),
            device_id_type=MESH,
        )

    def arrived(direction, hop, h):
        away = hop + 1 if direction == 0 else chips - hop - 1
        block = lax.rem(z + chips - away, chips) * 2 + core
        ref = acts_all.at[block, pl.ds(h * half, half), :]
        return ref, pltpu.make_async_copy(ref, ref, ring_recv.at[direction, hop, h])

    def to_pair(ref):
        pltpu.make_async_remote_copy(
            src_ref=ref,
            dst_ref=ref,
            send_sem=pair_sem.at[0],
            recv_sem=pair_sem.at[1],
            device_id=(r + 1 - 2 * core, e),
            device_id_type=MESH,
        ).start()

    far = chips // 2

    def goes(direction, hop, h):
        return hop < far - 1 or (hop == far - 1 and h == direction)

    ring_ops = [
        (direction, hop, h)
        for hop in range(far)
        for h in (0, 1)
        for direction in (0, 1)
        if goes(direction, hop, h)
    ]

    def spread(source, landing, sems):
        def body(k, _):
            to = lax.rem(e + k, owners)
            pltpu.make_async_remote_copy(
                src_ref=source(to),
                dst_ref=landing,
                send_sem=sems.at[0],
                recv_sem=sems.at[1],
                device_id=(r, to),
                device_id_type=MESH,
            ).start()
            return 0

        lax.fori_loop(1, owners, body, 0)
        pltpu.make_async_copy(source(e), landing, sems.at[1]).start()

    def wait_all(ref, sem):
        pltpu.make_async_copy(ref, ref, sem).wait()

    spread(lambda j: p_st.at[j], p_in.at[e], p_sem)
    for op in ring_ops:
        if op[1] == 0:
            ring(*op).start()
    to_pair(acts_all.at[r])
    send_rows(0)
    spread(lambda j: m_st.at[j], m_in.at[e], m_sem)

    wide = SUB * owners
    lane = lax.broadcasted_iota(jnp.int32, (SUB, wide), 1)
    sub = lax.broadcasted_iota(jnp.int32, (SUB, wide), 0)
    same_row = lax.rem(lane, SUB) == sub
    lane_expert = lane // SUB
    old_wide = jnp.zeros((SUB, wide), jnp.int32)
    rep_wide = jnp.zeros((SUB, wide), jnp.int32)
    for i in range(owners):
        old_wide = jnp.where(lane_expert == i, old_ref[i], old_wide)
        rep_wide = jnp.where(lane_expert == i, rep_ref[i], rep_wide)
    for d in range(owners):
        at = slice(d * SUB, (d + 1) * SUB)
        pick[at, :wide] = jnp.where(same_row & (old_wide == new_ref[d]), 1.0, 0.0)
        pick[at, wide:] = jnp.where(same_row & (rep_wide == new_ref[d]), 1.0, 0.0)

    def stack(block):
        return block.astype(F32).reshape(wide, LANES).astype(BF)

    def pass_on():
        wait_all(p_in, p_sem.at[1])
        move = pick[:, :wide].astype(BF)
        for t in range(rows // SUB):
            at = slice(t * SUB, (t + 1) * SUB)
            moved = jnp.dot(move, stack(p_in[:, at, :]), preferred_element_type=F32)
            p_out[:, at, :] = moved.reshape(owners, SUB, LANES).astype(BF)
        spread(lambda j: p_out.at[j], new_p.at[e], new_sem)

    for hop in range(far):
        for op in ring_ops:
            if op[1] != hop:
                continue
            direction, _, h = op
            ref, copy = arrived(*op)
            copy.wait()
            if hop + 1 < far and goes(direction, hop + 1, h):
                ring(direction, hop + 1, h).start()
            to_pair(ref)
        if hop == min(1, far - 1):
            pass_on()
        if hop == max(0, far - 2):
            for i in range(1, n_chunks):
                send_rows(i)
    for op in ring_ops:
        ring(*op).wait_send()
    mine = acts_all.at[pl.ds(0, chips)]
    wait_all(mine, pair_sem.at[1])

    def gradients(i):
        first, size = chunks[i]
        wait_all(g_buf[i], g_sem.at[i])
        width = groups * LANES
        block = g_buf[i][...].astype(F32).reshape(parts * size, width)
        in_own = lax.rem(lax.broadcasted_iota(jnp.int32, block.shape, 1), LANES) < LANES // 2
        left = jnp.concatenate(
            [jnp.where(in_own, block, 0.0).astype(BF), jnp.where(in_own, 0.0, block).astype(BF)], 0
        )
        for c0 in range(0, hidden, 256):
            n = min(256, hidden - c0)
            right = acts_all[:, :, c0 : c0 + n].reshape(groups * tokens, n)
            out = jnp.dot(left, right, preferred_element_type=F32)
            for slot in range(2):
                for q in range(parts):
                    at = (slot * parts + q) * size
                    for c in range(n // LANES):
                        piece = out[at : at + size, c * LANES : (c + 1) * LANES]
                        gs[i][q * cols + c0 // LANES + c, slot] = piece.astype(BF)
        spread(lambda j: gs[i].at[j], gi[i].at[e], gr_sem.at[i])

    def place():
        wait_all(m_in, m_sem.at[1])
        move = pick[:, :wide].astype(BF)
        for t in range(rows // SUB):
            at = slice(t * SUB, (t + 1) * SUB)
            both = jnp.concatenate([stack(m_in[:, item, at, :]) for item in range(2)], 1)
            placed[t] = jnp.dot(move, both, preferred_element_type=F32)

    def update(i):
        first, size = chunks[i]
        wait_all(gi[i], gr_sem.at[i, 1])
        both = pick[...].astype(BF)
        for t in range(size // SUB):
            at = slice(t * SUB, (t + 1) * SUB)
            terms = jnp.concatenate([stack(gi[i][:, item, at, :]) for item in range(2)], 0)
            gradient = jnp.dot(both, terms, preferred_element_type=F32)
            old = placed[first // SUB + t]
            first_old, second_old = old[:, :LANES], old[:, LANES:]
            first_new = beta_one * first_old + (1.0 - beta_one) * gradient
            second_new = beta_two * second_old + (1.0 - beta_two) * gradient * gradient
            for item, value in enumerate((first_new, second_new)):
                os_[i][:, item, at, :] = value.reshape(owners, SUB, LANES).astype(BF)
        spread(lambda j: os_[i].at[j], oi[i].at[e], out_sem.at[i])

    gradients(0)
    place()
    for i in range(1, n_chunks):
        gradients(i)
    for i in range(n_chunks):
        update(i)

    wait_all(new_p, new_sem.at[1])
    for i in range(n_chunks - 1):
        wait_all(oi[i], out_sem.at[i, 1])
        for q in range(parts):
            finish_part(chunks[i], q, cols, new_p, oi[i], results, chunks[i][0])

    others = pl.ds(0, owners - 1)
    wait_all(mine, pair_sem.at[0])
    wait_all(p_st.at[others], p_sem.at[0])
    wait_all(m_in.at[others], m_sem.at[0])
    wait_all(p_out.at[others], new_sem.at[0])
    for i in range(n_chunks):
        wait_all(g_buf[i].at[:, :, pl.ds(0, (groups - 1) * LANES)], rows_send.at[i])
        wait_all(gs[i].at[others], gr_sem.at[i, 0])
        wait_all(os_[i].at[others], out_sem.at[i, 0])
    wait_all(oi[n_chunks - 1], out_sem.at[n_chunks - 1, 1])


def finish(chunk, p_ref, moments_ref, *refs):
    done, outs, last, sems = refs[:3], refs[3:6], refs[6:9], refs[9]
    first, size = chunk
    parts, _, hidden = done[0].shape
    copies = []

    def copy(k, q, source, rows):
        target = outs[k].at[:, rows, :] if q == parts else outs[k].at[q, rows, :]
        copies.append(pltpu.make_async_copy(source, target, sems.at[k, q]))
        copies[-1].start()

    if first:
        for k in range(3):
            copy(k, parts, done[k].at[:, pl.ds(0, first), :], pl.ds(0, first))
    for q in range(parts):
        finish_part(chunk, q, hidden // LANES, p_ref, moments_ref, last, 0)
        for k in range(3):
            copy(k, q, last[k].at[q], pl.ds(first, size))
    for started in copies:
        started.wait()


def local(groups, owners, token_acts, out_grad, counts, params, first, second, old, rep, new):
    model_width, width = out_grad.shape[2:]
    slot_count, tok, hidden = token_acts.shape[2:]
    row_count = model_width // groups
    cols = hidden // LANES
    parts = owners // cols
    rows = row_count // parts
    chunks = splits(rows)
    block = (parts, rows, hidden)
    hbm = pl.BlockSpec(memory_space=pltpu.HBM)
    vmem = pl.BlockSpec(memory_space=pltpu.VMEM)
    n = len(chunks)
    wide = SUB * owners
    dma = pltpu.SemaphoreType.DMA
    operands = (
        token_acts.reshape(slot_count * tok, hidden),
        out_grad.reshape(groups, parts, rows, width),
        counts.reshape(slot_count),
        params.reshape(block),
        first.reshape(block),
        second.reshape(block),
        old,
        rep,
        new,
    )
    landed = pl.pallas_call(
        functools.partial(kernel, groups, owners),
        out_shape=[jax.ShapeDtypeStruct((owners, rows, LANES), BF)]
        + [jax.ShapeDtypeStruct((owners, 2, chunks[-1][1], LANES), BF)]
        + [jax.ShapeDtypeStruct(block, kind) for kind in (F32, BF, BF)],
        in_specs=[hbm] * len(operands),
        out_specs=[vmem] * 5,
        scratch_shapes=[
            pltpu.SMEM((slot_count,), jnp.int32),
            pltpu.SMEM((owners,), jnp.int32),
            pltpu.SMEM((owners,), jnp.int32),
            pltpu.SMEM((owners,), jnp.int32),
            pltpu.VMEM((groups, slot_count * tok, hidden), BF),
            pltpu.VMEM(block, F32),
            pltpu.VMEM(block, BF),
            pltpu.VMEM(block, BF),
            pltpu.VMEM((owners, rows, LANES), BF),
            pltpu.VMEM((owners, rows, LANES), BF),
            pltpu.VMEM((owners, rows, LANES), BF),
            pltpu.VMEM((owners, 2, rows, LANES), BF),
            pltpu.VMEM((owners, 2, rows, LANES), BF),
            pltpu.VMEM((wide, 2 * wide), F32),
            pltpu.VMEM((rows // SUB, wide, 2 * LANES), F32),
        ]
        + [pltpu.VMEM((parts, size, groups * LANES), BF) for _, size in chunks]
        + [pltpu.VMEM((owners, 2, size, LANES), BF) for _, size in chunks] * 3
        + [pltpu.VMEM((owners, 2, size, LANES), BF) for _, size in chunks[:-1]]
        + [
            dma((8,)),
            dma((n,)),
            dma((2, groups // 4, 2)),
            dma((2, groups // 4, 2)),
            dma((2,)),
            dma((n,)),
            dma((2,)),
            dma((2,)),
            dma((2,)),
            dma((n, 2)),
            dma((n, 2)),
        ],
        compiler_params=pltpu.CompilerParams(
            collective_id=0, has_side_effects=True, vmem_limit_bytes=36 * 1024 * 1024
        ),
    )(
        *(pltpu.with_memory_space_constraint(v, pltpu.HBM) for v in operands)
    )
    last = (parts, chunks[-1][1], hidden)
    out = pl.pallas_call(
        functools.partial(finish, chunks[-1]),
        out_shape=[jax.ShapeDtypeStruct(block, kind) for kind in (F32, BF, BF)],
        in_specs=[vmem] * 5,
        out_specs=[hbm] * 3,
        scratch_shapes=[pltpu.VMEM(last, kind) for kind in (F32, BF, BF)] + [dma((3, parts + 1))],
        compiler_params=pltpu.CompilerParams(vmem_limit_bytes=16 * 1024 * 1024),
    )(*landed)
    return tuple(x.reshape(1, row_count, hidden) for x in out)


def solution(mesh):
    return jax.shard_map(
        functools.partial(local, mesh.shape["edp"], mesh.shape["ep"]),
        mesh=mesh,
        in_specs=(
            P("edp", "ep", None, None, None),
            P("edp", "ep", None, None),
            P("edp", "ep", None),
            P("ep", "edp", None),
            P("ep", "edp", None),
            P("ep", "edp", None),
            P(),
            P(),
            P(),
        ),
        out_specs=(P("ep", "edp", None), P("ep", "edp", None), P("ep", "edp", None)),
        check_vma=False,
    )
```
